512 devices in a mesh: grp: 32 (over y, x), tp: 16 (over z, core).
Axes of the slice: x: 4, y: 8, z: 8, core: 2. Of those that a mesh axis runs over, the one named last changes fastest.
Arguments:
- tokens: bfloat16 [65536, 8192], P('grp', 'tp'), may hold values from -6 to 6
- base_weight: bfloat16 [8192, 2048], P('tp'), may hold values from -0.0625 to 0.0625
- down_tables: bfloat16 [4096, 8192, 16], P('grp', 'tp'), may hold values from -0.0625 to 0.0625
- up_tables: bfloat16 [4096, 16, 2048], P('grp', None, 'tp'), may hold values from -1.5 to 1.5
- block_owner: int32 [512, 1], P('grp'), may hold values from 0 to 31; in each aligned block of 16 rows (0 to 15, 16 to 31, ...) at most 2 rows name the same one
- block_local: int32 [512], P('grp'), may hold values from 0 to 127
- block_count: int32 [512], P('grp'), may hold values from 1 to 128
Outputs:
- projected: bfloat16 [65536, 2048], P('grp', 'tp')
The draws below stay inside these ranges and needn't reach their ends.
Inputs may be any that keep to these rules, and one draw needn't show every extreme that they name: `block_owner`: among the 16 blocks of one group (an aligned run of 16 entries) no owner is named more than 2 times, a bound that some block reaches.
All inputs are finite; a program needn't handle non-finite values.
Results may differ from the reference program's by a relative error of at most 0.001.
Values may be sent and summed in bfloat16 or wider, within the bound.
A program may use at most 64 MiB of HBM per device.

```python
import math
import jax
import jax.numpy as jnp
import numpy as np
from jax import lax

D = 8192
KEY_VALUE_COLUMNS = 2048
R = 16
BLOCK = 128
CAP = 2
ADP_GRP = 128
BLK_GRP = 16
GROUP_TOKEN_ROWS = 2048
ROWS = 65536
BLOCKS = 512
ADP = 4096
N_GRP = 32


def with_ends(drawn, own_key, low, top_value):
    spot = [jax.random.randint(jax.random.fold_in(own_key, axis), (), 0, length) for axis, length in enumerate(drawn.shape)]
    main_axis = drawn.shape.index(max(drawn.shape))
    neighbour = spot[:main_axis] + [(spot[main_axis] + 1) % drawn.shape[main_axis]] + spot[main_axis + 1:]
    return drawn.at[tuple(spot)].set(low).at[tuple(neighbour)].set(top_value)


def steps_of(rng, dims, cuts, least, top_value):
    def one(position, shards_of):
        steps = jax.random.uniform(jax.random.fold_in(jax.random.fold_in(rng, 6), position), (shards_of,), jnp.float32, least / len(cuts), top_value / len(cuts))
        return jnp.repeat(jnp.exp(steps), dims[position] // shards_of).reshape((-1,) + (1,) * (len(dims) - position - 1))

    loudness = one(*cuts[0])
    for cut in cuts[1:]:
        loudness = loudness * one(*cut)
    return loudness


def assign_block(rng, own, number, rows, count, top, limit, skew):
    sequence = jax.random.permutation(rng, count)
    packed, usual = shares(count, rows * top, limit, skew, True), shares(count, rows * top, limit, skew, False)
    places = jnp.arange(count)

    def named(tallies, turn):
        used = int((tallies > 0).sum())
        fixed = max(1, used // 4)
        passed = fixed + (places - fixed + turn * (used - fixed)) % max(1, count - fixed)
        return jnp.zeros((count,), jnp.int32).at[sequence[jnp.where(places < fixed, places, passed)]].set(jnp.asarray(tallies, jnp.int32))

    tallies = jnp.where(number % 4 == 0, named(packed, number // 4), named(usual, number - number // 4 - 1))
    mixed = jax.random.permutation(jax.random.fold_in(own, 3), count)
    donor, taker = mixed[0:count // 2 * 2:2], mixed[1:count // 2 * 2:2]
    margin = jnp.minimum(tallies[donor] - 1, limit - tallies[taker]) // 2
    margin = jnp.where((donor == sequence[0]) | (taker == sequence[0]) | (tallies[taker] == 0), 0, jnp.maximum(margin, 0))
    passed = jax.random.randint(jax.random.fold_in(own, 4), (count // 2,), 0, 1 << 20) % (margin + 1)
    tallies = tallies.at[donor].add(-passed).at[taker].add(passed)
    labels = jnp.searchsorted(jnp.cumsum(tallies), jnp.arange(rows * top), side="right").astype(jnp.int32)
    table = labels.reshape(top, rows).T
    table = table[jax.random.permutation(jax.random.fold_in(own, 1), rows)]
    turn = jax.random.randint(jax.random.fold_in(own, 2), (rows, 1), 0, top)
    return jnp.take_along_axis(table, (jnp.arange(top)[None, :] + turn) % top, axis=1)


def shares(amount, total, limit, lean, full):
    portions = [(1 << 20) // math.isqrt(rank ** lean) + 1 for rank in range(1, amount + 1)]
    largest = limit if full else min(limit, max(-(-total // amount), total * portions[0] // sum(portions)))
    least = 1 if total - largest >= amount - 1 else 0
    holding, surplus = [largest] + [least] * (amount - 1), total - largest - least * (amount - 1)
    while surplus > 0:
        free = [i for i in range(1, amount) if holding[i] < largest] or [i for i in range(1, amount) if holding[i] < limit]
        pool, remaining = sum([portions[i] for i in free]), surplus
        for i in free:
            extra = min(limit - holding[i], max(1, remaining * portions[i] // pool), surplus)
            holding[i] = holding[i] + extra
            surplus = surplus - extra
    return np.array(holding)


def centred(stream_key, extent, deviation, bound, shards=(), held_as=jnp.bfloat16):
    values = deviation * jax.random.normal(stream_key, extent, jnp.float32)
    if shards:
        values = values * steps_of(stream_key, extent, shards, -0.22, 0.18)
    return jnp.clip(values, -bound, bound).astype(held_as)


def setup_inputs(seed: int = 0) -> dict:
    streams_of = jax.random.split(jax.random.key(seed), 8)
    tokens = centred(streams_of[0], (ROWS, D), 1.0, 6.0, ((0, 32), (1, 16)))
    base_weight = centred(streams_of[1], (D, KEY_VALUE_COLUMNS), D ** -0.5, 0.0625, ((0, 16),))
    down_tables = centred(streams_of[2], (ADP, D, R), D ** -0.5, 0.0625, ((0, 32), (1, 16)))
    up_tables = centred(streams_of[3], (ADP, R, KEY_VALUE_COLUMNS), R ** -0.5, 1.5, ((0, 32), (2, 16)))
    block_owner_keys = jax.random.split(jax.random.fold_in(streams_of[4], 1), BLOCKS // BLK_GRP)
    block_owner_turns = jax.random.permutation(jax.random.fold_in(streams_of[4], 3), BLOCKS // BLK_GRP)
    block_owner = jax.vmap(lambda own, number: assign_block(jax.random.fold_in(streams_of[4], 2), own, number, BLK_GRP, N_GRP, 1, CAP, 2))(block_owner_keys, block_owner_turns).reshape((BLOCKS, 1))
    block_local = with_ends(jax.random.randint(streams_of[5], (BLOCKS,), 0, ADP_GRP), jax.random.fold_in(streams_of[5], 1), 0, ADP_GRP - 1).astype(jnp.int32)
    block_count = with_ends(jax.random.randint(streams_of[6], (BLOCKS,), 1, BLOCK + 1), jax.random.fold_in(streams_of[6], 1), 1, BLOCK).astype(jnp.int32)
    return dict(tokens=tokens, base_weight=base_weight, down_tables=down_tables, up_tables=up_tables, block_owner=block_owner, block_local=block_local, block_count=block_count)


adapter_scale = 2.0


def reference(tokens, base_weight, down_tables, up_tables, block_owner, block_local, block_count):
    adapter = (block_owner[:, 0] * ADP_GRP + block_local).astype(jnp.int32)
    weight_full = base_weight.astype(jnp.float32)

    def one_group(group):
        first_row = (group * GROUP_TOKEN_ROWS).astype(jnp.int32)
        first_block = (group * BLK_GRP).astype(jnp.int32)
        group_rows = lax.dynamic_slice_in_dim(tokens, first_row, GROUP_TOKEN_ROWS, 0).astype(jnp.float32)
        group_ids = lax.dynamic_slice_in_dim(adapter, first_block, BLK_GRP, 0)
        group_count = lax.dynamic_slice_in_dim(block_count, first_block, BLK_GRP, 0)
        base_projection = jnp.dot(group_rows, weight_full, preferred_element_type=jnp.float32)
        down_sel = jnp.take(down_tables, group_ids, axis=0).astype(jnp.float32)
        up_sel = jnp.take(up_tables, group_ids, axis=0).astype(jnp.float32)
        blocked = group_rows.reshape(BLK_GRP, BLOCK, D)
        reduced = jnp.einsum('nbd,ndr->nbr', blocked, down_sel)
        rank_reduced_state = jnp.einsum('nbr,nro->nbo', reduced, up_sel, precision=lax.Precision.HIGHEST)
        projection_total = base_projection + adapter_scale * rank_reduced_state.reshape(GROUP_TOKEN_ROWS, KEY_VALUE_COLUMNS)
        offsets = jnp.arange(BLOCK, dtype=jnp.int32)
        live_rows = (offsets[None, :] < group_count[:, None]).reshape(GROUP_TOKEN_ROWS, 1)
        return jnp.where(live_rows, projection_total, jnp.float32(0.0)).astype(jnp.bfloat16)

    stacked = lax.map(one_group, jnp.arange(N_GRP, dtype=jnp.int32))
    return stacked.reshape(ROWS, KEY_VALUE_COLUMNS)
```

```python
import functools

import jax
import jax.numpy as jnp
from jax import lax
from jax.experimental import pallas as pl
from jax.experimental.pallas import tpu as pltpu
from jax.sharding import PartitionSpec as P

R = 16
BLOCK = 128
CAP = 2
COLS = 128
CHUNK = 256
GROUPS = 8
LEVELS = 32766.0
adapter_scale = 2.0

OFFSETS = (4, 0, 3, 5, 2, 6, 1, 7)
PLUS, MINUS = 0, 1


def kernel(
    group_count, tokens, weight, down_table, up_table, owner, local, count, out,
    own_tokens, sib_tokens, own_weight, sib_weight, partial, send_q, recv_q, send_s, recv_s,
    table_d, table_u, send_d, recv_d, send_u, recv_u, id_send, id_recv, id_scalar, slot_scalar,
    rank_part, rank_recv, rank_sum, rank_full,
    load_sem, wload_sem, tok_send, tok_recv, w_send, w_recv, q_send, q_recv, s_send, s_recv,
    id_ssem, id_rsem, copy_sem, d_ssem, d_rsem, u_ssem, u_rsem, r_ssem, r_rsem, f_ssem, f_rsem,
):
    rows, feats = own_tokens.shape
    chunks = rows // CHUNK
    half = chunks // 2
    blocks = rows // BLOCK
    g = lax.axis_index("grp")
    t = lax.axis_index("tp")
    tp = lax.axis_size("tp")
    chips = tp // 2
    z = lax.div(t, 2)
    c = lax.rem(t, 2)
    sibling = 2 * z + 1 - c
    ring = (2 * lax.rem(z + 1, chips) + c, 2 * lax.rem(z + chips - 1, chips) + c)

    barrier = pltpu.get_barrier_semaphore()

    def greet_group(k, carry):
        pl.semaphore_signal(barrier, inc=1, device_id={"grp": lax.rem(g + k, group_count)})
        return carry

    def greet_tp(k, carry):
        pl.semaphore_signal(barrier, inc=1, device_id={"tp": lax.rem(t + k, tp)})
        return carry

    lax.fori_loop(1, group_count, greet_group, 0)
    lax.fori_loop(1, tp, greet_tp, 0)

    load_tokens = pltpu.make_async_copy(tokens, own_tokens, load_sem.at[0])
    load_down = pltpu.make_async_copy(down_table, table_d, load_sem.at[1])
    load_up = pltpu.make_async_copy(up_table, table_u, load_sem.at[2])

    def weight_block(slot, core):
        column = (lax.rem(z + OFFSETS[slot], chips) * 2 + core) * COLS
        return weight.at[:, pl.ds(pl.multiple_of(column, COLS), COLS)]

    load_weight = [
        pltpu.make_async_copy(weight_block(j, c), own_weight.at[:, pl.ds(j * COLS, COLS)], wload_sem.at[j])
        for j in range(8)
    ]
    load_weight[0].start()
    load_weight[1].start()
    load_tokens.start()
    for j in range(2, 8):
        load_weight[j].start()
    load_down.start()
    load_up.start()

    lanes = lax.broadcasted_iota(jnp.int32, (8, 128), 1)
    wanted = jnp.zeros((8, 128), jnp.int32)
    owners = [owner[n] for n in range(blocks)]
    for n in range(blocks):
        earlier = jnp.int32(0)
        for m in range(n):
            earlier = earlier + (owners[m] == owners[n]).astype(jnp.int32)
        slot = owners[n] * CAP + earlier
        slot_scalar[n] = slot
        wanted = jnp.where(lanes == slot, local[n], wanted)
    id_send[...] = wanted
    id_recv[g] = wanted

    pl.semaphore_wait(barrier, group_count - 1 + tp - 1)

    def send_ids(k, carry):
        pltpu.make_async_remote_copy(
            src_ref=id_send, dst_ref=id_recv.at[g], send_sem=id_ssem, recv_sem=id_rsem,
            device_id={"grp": lax.rem(g + k, group_count)},
        ).start()
        return carry

    lax.fori_loop(1, group_count, send_ids, 0)

    def swap_weight(j):
        return pltpu.make_async_remote_copy(
            src_ref=weight_block(j, 1 - c), dst_ref=sib_weight.at[:, pl.ds(j * COLS, COLS)],
            send_sem=w_send.at[j], recv_sem=w_recv.at[j], device_id={"tp": sibling},
        )

    def chunk_rows(r):
        return pl.ds(pl.multiple_of(r * CHUNK, CHUNK), CHUNK)

    def swap_tokens(r):
        return pltpu.make_async_remote_copy(
            src_ref=tokens.at[chunk_rows(r)], dst_ref=sib_tokens.at[chunk_rows(r)],
            send_sem=tok_send.at[r], recv_sem=tok_recv.at[r], device_id={"tp": sibling},
        )

    swap_weight(0).start()
    swap_weight(1).start()
    for i in range(half):
        swap_tokens(i).start()
        swap_tokens(half + i).start()
    for j in range(2, 8):
        swap_weight(j).start()

    def data_copy(d, s, r):
        return pltpu.make_async_remote_copy(
            src_ref=send_q.at[d, s, chunk_rows(r)], dst_ref=recv_q.at[d, s, chunk_rows(r)],
            send_sem=q_send.at[d, s, r], recv_sem=q_recv.at[d, s, r], device_id={"tp": ring[d]},
        )

    def scale_copy(d, s, r):
        return pltpu.make_async_remote_copy(
            src_ref=send_s.at[d, s, r], dst_ref=recv_s.at[d, s, r],
            send_sem=s_send.at[d, s, r], recv_sem=s_recv.at[d, s, r], device_id={"tp": ring[d]},
        )

    def pass_on(d, s, r, value):
        grouped = value.reshape(GROUPS, CHUNK // GROUPS, COLS)
        top = jnp.maximum(jnp.max(jnp.abs(grouped), axis=1), 1e-30)
        send_s[d, s, r] = top * (1.0 / LEVELS)
        coded = jnp.round(grouped * (LEVELS / top)[:, None, :])
        send_q[d, s, chunk_rows(r)] = coded.astype(jnp.int32).astype(jnp.int16).reshape(CHUNK, COLS)
        scale_copy(d, s, r).start()
        data_copy(d, s, r).start()

    def arrived(d, s, r):
        scale_copy(d, s, r).wait_recv()
        data_copy(d, s, r).wait_recv()
        value = recv_q[d, s, chunk_rows(r)].astype(jnp.int32).astype(jnp.float32)
        value = value.reshape(GROUPS, CHUNK // GROUPS, COLS) * recv_s[d, s, r][:, None, :]
        return value.reshape(CHUNK, COLS)

    def product(pair, r):
        columns = pl.ds(pair * 2 * COLS, 2 * COLS)
        return jnp.dot(
            own_tokens[chunk_rows(r)], own_weight[:, columns], preferred_element_type=jnp.float32
        ) + jnp.dot(
            sib_tokens[chunk_rows(r)], sib_weight[:, columns], preferred_element_type=jnp.float32
        )

    load_weight[0].wait()
    load_weight[1].wait()
    load_tokens.wait()
    swap_weight(0).wait_recv()
    swap_weight(1).wait_recv()

    def far_half(d, r):
        swap_tokens(r).wait_recv()
        both = product(0, r)
        partial[1, chunk_rows(r)] = both[:, COLS:]
        pass_on(d, 0, r, both[:, :COLS])

    def far_step(i, carry):
        far_half(PLUS, i)
        far_half(MINUS, half + i)
        return carry

    lax.fori_loop(0, half, far_step, 0)

    all_ids = id_recv.at[pl.ds(0, group_count - 1)]
    pltpu.make_async_copy(all_ids, all_ids, id_rsem).wait()
    fetch_ids = pltpu.make_async_copy(id_recv.at[:, 0], id_scalar, copy_sem)
    fetch_ids.start()
    load_down.wait()
    load_up.wait()
    fetch_ids.wait()

    for r in range(CAP):
        mine = id_scalar[g, CAP * g + r]
        recv_d[CAP * g + r] = table_d[mine]
        recv_u[CAP * g + r] = table_u[mine]

    def pair_of(index):
        return pl.ds(index * CAP, CAP)

    def send_down(k, carry):
        peer = lax.rem(g + k, group_count)
        for r in range(CAP):
            send_d[CAP * peer + r] = table_d[id_scalar[peer, CAP * g + r]]
        pltpu.make_async_remote_copy(
            src_ref=send_d.at[pair_of(peer)], dst_ref=recv_d.at[pair_of(g)],
            send_sem=d_ssem, recv_sem=d_rsem, device_id={"grp": peer},
        ).start()
        return carry

    def send_up(k, carry):
        peer = lax.rem(g + k, group_count)
        for r in range(CAP):
            send_u[CAP * peer + r] = table_u[id_scalar[peer, CAP * g + r]]
        pltpu.make_async_remote_copy(
            src_ref=send_u.at[pair_of(peer)], dst_ref=recv_u.at[pair_of(g)],
            send_sem=u_ssem, recv_sem=u_rsem, device_id={"grp": peer},
        ).start()
        return carry

    lax.fori_loop(1, group_count, send_down, 0)
    lax.fori_loop(1, group_count, send_up, 0)

    def fill(pair):
        for j in (2 * pair, 2 * pair + 1):
            load_weight[j].wait()
            swap_weight(j).wait_recv()

        def one(r, carry):
            both = product(pair, r)
            partial[2 * pair, chunk_rows(r)] = both[:, :COLS]
            partial[2 * pair + 1, chunk_rows(r)] = both[:, COLS:]
            return carry

        lax.fori_loop(0, chunks, one, 0)

    def first_hop(i, carry):
        low, high = i, half + i
        pass_on(PLUS, 1, high, partial[2, chunk_rows(high)])
        pass_on(MINUS, 1, low, partial[3, chunk_rows(low)])
        return carry

    def first_sum(i, carry):
        low, high = i, half + i
        pass_on(PLUS, 1, low, partial[2, chunk_rows(low)] + arrived(PLUS, 0, low))
        pass_on(MINUS, 1, high, partial[3, chunk_rows(high)] + arrived(MINUS, 0, high))
        return carry

    def hop(s):
        def one(i, carry):
            high = lax.rem(i + half, chunks)
            pass_on(PLUS, s, high, partial[2 * s, chunk_rows(high)] + arrived(PLUS, s - 1, high))
            pass_on(MINUS, s, i, partial[2 * s + 1, chunk_rows(i)] + arrived(MINUS, s - 1, i))
            return carry

        lax.fori_loop(0, chunks, one, 0)

    fill(1)
    lax.fori_loop(0, half, first_hop, 0)
    fill(2)
    lax.fori_loop(0, half, first_sum, 0)
    fill(3)
    hop(2)
    hop(3)

    others_d = recv_d.at[pl.ds(0, CAP * (group_count - 1))]
    pltpu.make_async_copy(others_d, others_d, d_rsem).wait()

    def block_rows(n):
        return pl.ds(pl.multiple_of(n * BLOCK, BLOCK), BLOCK)

    def reduce_block(n, carry):
        rank_part[n] = lax.dot_general(
            recv_d[slot_scalar[n]], own_tokens[block_rows(n)], (((1,), (1,)), ((), ())),
            preferred_element_type=jnp.float32,
        )
        return carry

    lax.fori_loop(0, blocks, reduce_block, 0)

    def scatter_rank(k, carry):
        peer = lax.rem(t + k, tp)
        pltpu.make_async_remote_copy(
            src_ref=rank_part.at[peer], dst_ref=rank_recv.at[t],
            send_sem=r_ssem, recv_sem=r_rsem, device_id={"tp": peer},
        ).start()
        return carry

    lax.fori_loop(1, tp, scatter_rank, 0)
    rank_recv[t] = rank_part[t]
    others_r = rank_recv.at[pl.ds(0, tp - 1)]
    pltpu.make_async_copy(others_r, others_r, r_rsem).wait()
    total = jnp.sum(rank_recv[...], axis=0)
    rank_sum[...] = total
    rank_full[t] = total

    def gather_rank(k, carry):
        pltpu.make_async_remote_copy(
            src_ref=rank_sum, dst_ref=rank_full.at[t],
            send_sem=f_ssem, recv_sem=f_rsem, device_id={"tp": lax.rem(t + k, tp)},
        ).start()
        return carry

    lax.fori_loop(1, tp, gather_rank, 0)

    def last_sum(i, carry):
        high = lax.rem(i + half, chunks)
        partial[1, chunk_rows(high)] += arrived(PLUS, 3, high)
        partial[1, chunk_rows(i)] += arrived(MINUS, 3, i)
        return carry

    lax.fori_loop(0, chunks, last_sum, 0)

    others_u = recv_u.at[pl.ds(0, CAP * (group_count - 1))]
    pltpu.make_async_copy(others_u, others_u, u_rsem).wait()
    pltpu.make_async_copy(others_r, others_r, f_rsem).wait()
    offsets = lax.broadcasted_iota(jnp.int32, (BLOCK, COLS), 0)

    def finish(n, carry):
        lowrank = lax.dot_general(
            rank_full[n], recv_u[slot_scalar[n]].astype(jnp.float32), (((0,), (0,)), ((), ())),
            precision=lax.Precision.HIGHEST, preferred_element_type=jnp.float32,
        )
        value = partial[1, block_rows(n)] + adapter_scale * lowrank
        out[block_rows(n)] = jnp.where(offsets < count[n], value, 0.0).astype(out.dtype)
        return carry

    lax.fori_loop(0, blocks, finish, 0)

    def sent_far(i, carry):
        for d, r in ((PLUS, i), (MINUS, half + i)):
            data_copy(d, 0, r).wait_send()
            scale_copy(d, 0, r).wait_send()
        return carry

    lax.fori_loop(0, half, sent_far, 0)

    def sent_chunk(r, carry):
        for d in (PLUS, MINUS):
            for s in (1, 2, 3):
                data_copy(d, s, r).wait_send()
                scale_copy(d, s, r).wait_send()
        swap_tokens(r).wait_send()
        return carry

    lax.fori_loop(0, chunks, sent_chunk, 0)
    for j in range(8):
        swap_weight(j).wait_send()
    pltpu.make_async_copy(all_ids, all_ids, id_ssem).wait()
    pltpu.make_async_copy(others_d, others_d, d_ssem).wait()
    pltpu.make_async_copy(others_u, others_u, u_ssem).wait()
    pltpu.make_async_copy(others_r, others_r, r_ssem).wait()
    pltpu.make_async_copy(others_r, others_r, f_ssem).wait()


def body(tokens, base_weight, down_tables, up_tables, block_owner, block_local, block_count):
    group_count = lax.axis_size("grp")
    tp = lax.axis_size("tp")
    rows, feats = tokens.shape
    adapters = down_tables.shape[0]
    chunks = rows // CHUNK
    blocks = rows // BLOCK
    slots = CAP * group_count
    bf16, f32, i32 = jnp.bfloat16, jnp.float32, jnp.int32
    dma = pltpu.SemaphoreType.DMA
    vmem = pltpu.VMEM
    anywhere = pl.BlockSpec(memory_space=pl.ANY)
    scalar = pl.BlockSpec(memory_space=pltpu.SMEM)
    return pl.pallas_call(
        functools.partial(kernel, group_count),
        out_shape=jax.ShapeDtypeStruct((rows, COLS), bf16),
        in_specs=[anywhere] * 4 + [scalar] * 3,
        out_specs=pl.BlockSpec(memory_space=pltpu.VMEM),
        scratch_shapes=[
            vmem((rows, feats), bf16), vmem((rows, feats), bf16),
            vmem((feats, 8 * COLS), bf16), vmem((feats, 8 * COLS), bf16),
            vmem((8, rows, COLS), f32),
            vmem((2, 4, rows, COLS), jnp.int16), vmem((2, 4, rows, COLS), jnp.int16),
            vmem((2, 4, chunks, GROUPS, COLS), f32), vmem((2, 4, chunks, GROUPS, COLS), f32),
            vmem((adapters, R, feats), bf16), vmem((adapters, R, COLS), bf16),
            vmem((slots, R, feats), bf16), vmem((slots, R, feats), bf16),
            vmem((slots, R, COLS), bf16), vmem((slots, R, COLS), bf16),
            vmem((8, 128), i32), vmem((group_count, 8, 128), i32),
            pltpu.SMEM((group_count, 128), i32), pltpu.SMEM((blocks,), i32),
            vmem((blocks, R, BLOCK), f32), vmem((tp, R, BLOCK), f32),
            vmem((R, BLOCK), f32), vmem((blocks, R, BLOCK), f32),
            dma((3,)), dma((8,)), dma((chunks,)), dma((chunks,)), dma((8,)), dma((8,)),
            dma((2, 4, chunks)), dma((2, 4, chunks)), dma((2, 4, chunks)), dma((2, 4, chunks)),
            dma, dma, dma, dma, dma, dma, dma, dma, dma, dma, dma,
        ],
        compiler_params=pltpu.CompilerParams(
            collective_id=0, has_side_effects=True, vmem_limit_bytes=56 * 2**20
        ),
    )(
        tokens, base_weight, jnp.transpose(down_tables, (0, 2, 1)), up_tables,
        block_owner[:, 0], block_local, block_count,
    )


def solution(mesh):
    placed = (
        P("grp", "tp"),
        P("tp", None),
        P("grp", "tp", None),
        P("grp", None, "tp"),
        P("grp", None),
        P("grp"),
        P("grp"),
    )
    return jax.shard_map(
        body, mesh=mesh, in_specs=placed, out_specs=P("grp", "tp"), check_vma=False
    )
```
